256 devices in a mesh: dp: 32 (over z, x), tensor: 8 (over y, core).
Axes of the slice: x: 4, y: 4, z: 8, core: 2. Of those that a mesh axis runs over, the one named last changes fastest.
Arguments:
- tokens: bfloat16 [65536, 8192], P('dp', 'tensor'), may hold values from -6 to 6
- base_value_weight: bfloat16 [8192, 1024], P('tensor'), may hold values from -0.0625 to 0.0625
- adapter_down_weight: bfloat16 [512, 8192, 64], P('dp', 'tensor'), may hold values from -0.0625 to 0.0625
- adapter_up_weight: bfloat16 [512, 64, 1024], P('dp', None, 'tensor'), may hold values from -0.75 to 0.75
- request_adapter_index: int32 [128], P('dp'), may hold values from 0 to 511
- storage_index_table: int32 [512], replicated, may hold values from 0 to 511, each once
Outputs:
- values_out: bfloat16 [65536, 1024], P('dp', 'tensor')
The draws below stay inside these ranges and needn't reach their ends.
Inputs may be any that keep to these rules, and one draw needn't show every extreme that they name: `request_adapter_index`: each adapter id names an adapter. storage_index_table is a permutation of the storage positions.
All inputs are finite; a program needn't handle non-finite values.
Results may differ from the reference program's by a relative error of at most 0.003.
Values may be sent and summed in bfloat16 or wider, within the bound.
A program may use at most 128 MiB of HBM per device.

```python
import math
import jax
import jax.numpy as jnp
import numpy as np
from jax import lax

MODEL_WIDTH = 8192
VALUE_FEATURES = 1024
ADAPTER_RANK = 64
SEQ = 512
REQUESTS = 128
TOKENS = 65536
ADAPTER_TOTAL = 512


def set_ends(result, own_key, low, high):
    extent = result.shape
    spot = [jax.random.randint(jax.random.fold_in(own_key, axis), (), 0, extent[axis]) for axis in range(len(extent))]
    result = result.at[tuple(spot)].set(low)
    longest = extent.index(max(extent))
    spot[longest] = (spot[longest] + 1) % extent[longest]
    return result.at[tuple(spot)].set(high)


def level_of(key, shape, cuts, least, high):
    level = 1.0
    for position, shards_of in cuts:
        steps = jax.random.uniform(jax.random.fold_in(jax.random.fold_in(key, 6), position), (shards_of,), jnp.float32, least / len(cuts), high / len(cuts))
        level = level * jnp.repeat(jnp.exp(steps), shape[position] // shards_of).reshape((-1,) + (1,) * (len(shape) - 1 - position))
    return level


def rank_table(count, slope):
    loads = [(1 << 20) // math.isqrt(rank ** slope) + 1 for rank in range(1, count + 1)]
    width = 1 + sum(loads) // (1 << 30)
    return np.cumsum(np.array([max(1, weight // width) for weight in loads]))


def ranked(stream_key, extent, amount, lean):
    listing = rank_table(amount, lean)
    pick = jax.random.randint(jax.random.fold_in(stream_key, 1), extent, 0, int(listing[amount - 1]))
    rank = jnp.searchsorted(jnp.asarray(listing, jnp.int32), pick, side="right")
    return jax.random.permutation(jax.random.fold_in(stream_key, 2), amount)[rank].astype(jnp.int32)


def normal_values(own_key, shape, spread, bound, split=(), dtype=jnp.bfloat16):
    result = spread * jax.random.normal(own_key, shape, jnp.float32)
    if split:
        result = result * level_of(own_key, shape, split, -0.22, 0.18)
    return jnp.clip(result, -bound, bound).astype(dtype)


def setup_inputs(seed: int = 0) -> dict:
    keys = jax.random.split(jax.random.key(seed), 7)
    tokens = normal_values(keys[0], (TOKENS, MODEL_WIDTH), 1.0, 6.0, ((0, 32), (1, 8)))
    base_value_weight = normal_values(keys[1], (MODEL_WIDTH, VALUE_FEATURES), MODEL_WIDTH ** -0.5, 0.0625, ((0, 8),))
    adapter_down_weight = normal_values(keys[2], (ADAPTER_TOTAL, MODEL_WIDTH, ADAPTER_RANK), MODEL_WIDTH ** -0.5, 0.0625, ((0, 32), (1, 8)))
    adapter_up_weight = normal_values(keys[3], (ADAPTER_TOTAL, ADAPTER_RANK, VALUE_FEATURES), ADAPTER_RANK ** -0.5, 0.75, ((0, 32), (2, 8)))
    request_adapter_index = set_ends(ranked(keys[4], (REQUESTS,), ADAPTER_TOTAL, 2), jax.random.fold_in(keys[4], 3), 0, ADAPTER_TOTAL - 1).astype(jnp.int32)
    storage_index_table = jax.random.permutation(keys[5], ADAPTER_TOTAL).astype(jnp.int32)
    return dict(tokens=tokens, base_value_weight=base_value_weight, adapter_down_weight=adapter_down_weight, adapter_up_weight=adapter_up_weight, request_adapter_index=request_adapter_index, storage_index_table=storage_index_table)


adapter_scale = 0.5


def reference(tokens, base_value_weight, adapter_down_weight, adapter_up_weight, request_adapter_index, storage_index_table):
    base_output = jnp.dot(tokens, base_value_weight, preferred_element_type=jnp.float32)
    grouped = tokens.reshape(REQUESTS, SEQ, MODEL_WIDTH)
    positions = storage_index_table[request_adapter_index].astype(jnp.int32)

    def one_request(item):
        rows, storage_index = item
        down_projected = adapter_down_weight[storage_index]
        up_projected = adapter_up_weight[storage_index]
        low = jnp.dot(rows, down_projected, preferred_element_type=jnp.float32).astype(jnp.bfloat16)
        return jnp.dot(low, up_projected, preferred_element_type=jnp.float32)

    adapter_update = lax.map(one_request, (grouped, positions)).reshape(TOKENS, VALUE_FEATURES)
    return (base_output + adapter_scale * adapter_update).astype(jnp.bfloat16)
```

```python
import jax
import jax.numpy as jnp
from jax import lax
from jax.sharding import PartitionSpec as P

adapter_scale = 0.5


def shards(
    tokens,
    base_value_weight,
    adapter_down_weight,
    adapter_up_weight,
    request_adapter_index,
    storage_index_table,
):
    n_rows, width = tokens.shape
    requests_here = request_adapter_index.shape[0]
    seq_len = n_rows // requests_here
    owned = adapter_down_weight.shape[0]
    rank = adapter_down_weight.shape[2]
    local_columns = adapter_up_weight.shape[2]
    n_dp = lax.axis_size("dp")

    down_t = jnp.swapaxes(adapter_down_weight, 1, 2)
    pieces = jnp.concatenate(
        (
            down_t.reshape(owned, n_dp, rank * width // n_dp // 128, 128),
            adapter_up_weight.reshape(owned, n_dp, rank * local_columns // n_dp // 128, 128),
        ),
        axis=2,
    )
    pieces = jnp.swapaxes(pieces, 0, 1)
    held = lax.all_to_all(pieces, "dp", split_axis=0, concat_axis=0, tiled=True)
    held = held.reshape(n_dp * owned, -1, 128)

    every_id = lax.all_gather(request_adapter_index, "dp", axis=0, tiled=True)
    positions = storage_index_table[every_id]
    outgoing = held[positions].reshape(n_dp, requests_here, -1, 128)
    fetched = lax.all_to_all(outgoing, "dp", split_axis=0, concat_axis=0, tiled=True)
    fetched = jnp.swapaxes(fetched, 0, 1)
    down_rows = rank * width // n_dp // 128
    down_sel = fetched[:, :, :down_rows].reshape(requests_here, rank, width)
    up_sel = fetched[:, :, down_rows:].reshape(requests_here, rank, local_columns)

    base_projection = lax.psum_scatter(
        lax.dot_general(
            base_value_weight, tokens, (((0,), (1,)), ((), ())), preferred_element_type=jnp.float32
        ),
        "tensor",
        scatter_dimension=0,
        tiled=True,
    ).T

    grouped = tokens.reshape(requests_here, seq_len, width)
    low_part = jnp.einsum("rsd,rkd->rks", grouped, down_sel, preferred_element_type=jnp.float32)
    low = lax.psum(low_part, "tensor").astype(jnp.bfloat16)
    adapter_update = jnp.einsum("rks,rkc->rsc", low, up_sel, preferred_element_type=jnp.float32)
    adapter_update = adapter_update.reshape(n_rows, local_columns)
    return (base_projection + adapter_scale * adapter_update).astype(jnp.bfloat16)


def solution(mesh):
    return jax.shard_map(
        shards,
        mesh=mesh,
        in_specs=(
            P("dp", "tensor"),
            P("tensor", None),
            P("dp", "tensor", None),
            P("dp", None, "tensor"),
            P("dp"),
            P(),
        ),
        out_specs=P("dp", "tensor"),
        check_vma=False,
    )
```

```python
import functools

import jax
import jax.numpy as jnp
from jax import lax
from jax.experimental import pallas as pl
from jax.experimental.pallas import tpu as pltpu
from jax.sharding import PartitionSpec as P

MESH = pl.DeviceIdType.MESH
adapter_scale = 0.5
LANES = 128
ROWS = 16
SLOTS = 4
VMEM_LIMIT = 60 * 1024 * 1024


def iota(shape, axis):
    return lax.broadcasted_iota(jnp.int32, shape, axis)


def visit(q, n):
    half = q // 2 + 1
    return half + (q % 2) * (n - 2 * half)


def ids_kernel(n_dp, owned, upr, ids_ref, table_ref, row_ref, col_ref, mine, every, send_sem, recv_sem):
    dp = lax.axis_index("dp")
    shift = owned.bit_length() - 1
    rp = SLOTS * upr
    slot = iota((rp, LANES), 0) // upr
    tile = jnp.zeros((rp, LANES), jnp.int32)
    for s in range(SLOTS):
        tile = jnp.where(slot == s, ids_ref[s], tile)
    mine[...] = tile
    every[dp] = tile

    barrier = pltpu.get_barrier_semaphore()

    def greet(q, _):
        peer = lax.rem(dp + q, n_dp)
        pl.semaphore_signal(barrier, inc=1, device_id={"dp": peer}, device_id_type=MESH)
        return 0

    lax.fori_loop(1, n_dp, greet, 0)
    pl.semaphore_wait(barrier, n_dp - 1)

    def push(step):
        return pltpu.make_async_remote_copy(
            src_ref=mine,
            dst_ref=every.at[dp],
            send_sem=send_sem.at[step],
            recv_sem=recv_sem.at[step],
            device_id={"dp": lax.rem(dp + step, n_dp)},
            device_id_type=MESH,
        )

    def go(step, _):
        push(step).start()
        return 0

    def come(step, _):
        push(step).wait()
        return 0

    lax.fori_loop(1, n_dp, go, 0)
    lax.fori_loop(1, n_dp, come, 0)

    n = n_dp * rp
    ids = every[...].reshape(n, LANES)
    blocks = table_ref.shape[1] // LANES
    lane = iota((n, LANES), 1)
    pos = jnp.zeros((n, 1), jnp.int32)
    for b in range(blocks):
        row = table_ref[:, b * LANES : (b + 1) * LANES]
        hit = ids == lane + b * LANES
        pos += jnp.sum(jnp.where(hit, row, 0), axis=1, keepdims=True)
    owner = lax.shift_right_logical(pos, shift)
    rank = jnp.zeros((n, 1), jnp.int32)
    count = jnp.zeros((n, 1), jnp.int32)
    for b in range(blocks):
        at = lane + b * LANES
        needed = jnp.max(jnp.where(pos == at, 1, 0), axis=0, keepdims=True)
        same = jnp.where(lax.shift_right_logical(at, shift) == owner, needed, 0)
        count += jnp.sum(same, axis=1, keepdims=True)
        rank += jnp.sum(jnp.where(at < pos, same, 0), axis=1, keepdims=True)
    code = owner * owned + rank
    col_ref[...] = jnp.broadcast_to(code, (n, LANES))
    for b in range(n // LANES):
        diag = iota((n, LANES), 0) == lane + b * LANES
        row_ref[0:1, b * LANES : (b + 1) * LANES] = jnp.sum(jnp.where(diag, code, 0), axis=0, keepdims=True)
    own = jnp.where((owner == dp) & (rank == lane), pos - dp * owned, 0)
    row_ref[1:2, 0:LANES] = jnp.max(own, axis=0, keepdims=True)
    row_ref[2:3, 0:LANES] = jnp.broadcast_to(jnp.max(count, axis=0, keepdims=True), (1, LANES))


def main_kernel(
    n_dp, n_t, k, upr,
    row_ref, col_ref, tok_hbm, w_hbm, down_hbm, up_hbm, out_ref,
    tok, w, down, up, upt, stage, held, outb, land, part, pair, anti, fwd, bwd, hop_a, hop_b, got_f, got_b,
    panel, lowp, lowr, lowb, lowa,
    load_sem, s1, r1, s2, r2, sp, rp_, sh, rh, s3, r3, s4, r4,
):
    dp = lax.axis_index("dp")
    t = lax.axis_index("tensor")
    y, c = t // 2, t % 2
    n_y = n_t // 2
    n_rows, width = tok.shape
    owned, rank, _ = down.shape
    seq = n_rows // SLOTS
    ncg = width // LANES
    nu = -(-upr * k // ROWS)
    nt = k + nu
    nuo = -(-SLOTS * upr // ROWS)
    no = SLOTS + nuo
    rp = SLOTS * upr
    half = n_rows // 2
    tb = n_rows // n_t

    loads = [
        pltpu.make_async_copy(a, b, load_sem.at[i])
        for i, (a, b) in enumerate(((down_hbm, down), (up_hbm, up), (tok_hbm, tok), (w_hbm, w)))
    ]
    for cp in loads:
        cp.start()

    barrier = pltpu.get_barrier_semaphore()

    def greet_dp(q, _):
        pl.semaphore_signal(barrier, inc=1, device_id={"dp": lax.rem(dp + q, n_dp)}, device_id_type=MESH)
        return 0

    def greet_t(q, _):
        pl.semaphore_signal(barrier, inc=1, device_id={"tensor": lax.rem(t + q, n_t)}, device_id_type=MESH)
        return 0

    lax.fori_loop(1, n_dp, greet_dp, 0)
    lax.fori_loop(1, n_t, greet_t, 0)

    loads[0].wait()
    loads[1].wait()

    def pick(j, _):
        which = row_ref[1, j]
        for i in range(n_dp):
            rg, cg = divmod(i, ncg)
            stage[i * nt + j] = down[which, rg * ROWS : (rg + 1) * ROWS, cg * LANES : (cg + 1) * LANES]
        return 0

    lax.fori_loop(0, k, pick, 0)
    kk = nu * ROWS // upr
    for j in range(kk):
        upt[j * rank : (j + 1) * rank, :] = up[row_ref[1, min(j, k - 1)]]
    m = n_dp * nu * ROWS
    r = iota((m, kk * rank), 0)
    src = (r % (nu * ROWS)) // upr * rank + r // (nu * ROWS) * upr + r % upr
    perm = jnp.where(src == iota((m, kk * rank), 1), 1.0, 0.0).astype(jnp.bfloat16)
    ups = jnp.dot(perm, upt[0 : kk * rank, :], preferred_element_type=jnp.float32).astype(jnp.bfloat16)
    for i in range(n_dp):
        for u in range(nu):
            b = i * nu + u
            stage[i * nt + k + u] = ups[b * ROWS : (b + 1) * ROWS, :]

    pl.semaphore_wait(barrier, n_dp - 1 + n_t - 1)

    def exchange(src_ref, dst_ref, size, send_sem, recv_sem, step):
        peer = lax.rem(dp + step, n_dp)
        return pltpu.make_async_remote_copy(
            src_ref=src_ref.at[pl.ds(peer * size, size)],
            dst_ref=dst_ref.at[pl.ds(dp * size, size)],
            send_sem=send_sem.at[step],
            recv_sem=recv_sem.at[step],
            device_id={"dp": peer},
            device_id_type=MESH,
        )

    def start_all(make):
        def body(q, _):
            make(visit(q, n_dp)).start()
            return 0

        lax.fori_loop(0, n_dp - 1, body, 0)

    def wait_all(make, kind):
        def body(q, _):
            cp = make(visit(q, n_dp))
            cp.wait_recv() if kind == "recv" else cp.wait_send()
            return 0

        lax.fori_loop(0, n_dp - 1, body, 0)

    first = functools.partial(exchange, stage, held, nt, s1, r1)
    second = functools.partial(exchange, outb, land, no, s2, r2)

    start_all(first)

    def keep1(b, _):
        held[dp * nt + b] = stage[dp * nt + b]
        return 0

    lax.fori_loop(0, nt, keep1, 0)

    loads[2].wait()
    loads[3].wait()

    def to_tensor(src_ref, dst_ref, send_sem, recv_sem, peer):
        return pltpu.make_async_remote_copy(
            src_ref=src_ref, dst_ref=dst_ref, send_sem=send_sem, recv_sem=recv_sem,
            device_id={"tensor": peer}, device_id_type=MESH,
        )

    partner = t + 1 - 2 * c
    own_cols = pl.ds(pl.multiple_of(c * LANES, LANES), LANES)
    other_cols = pl.ds(pl.multiple_of((1 - c) * LANES, LANES), LANES)
    mb = 256
    pairs = {}
    for rel in (2, 1, 3, 0):
        target = lax.rem(y + rel, n_y)
        cols = pl.ds(pl.multiple_of(target * 2 * LANES, 2 * LANES), 2 * LANES)

        def block(i, _, rel=rel, cols=cols):
            rows = pl.ds(pl.multiple_of(i * mb, mb), mb)
            part[rel, rows, :] = jnp.dot(tok[rows, :], w[:, cols], preferred_element_type=jnp.float32)
            return 0

        lax.fori_loop(0, n_rows // mb, block, 0)
        pairs[rel] = to_tensor(part.at[rel, :, other_cols], pair.at[rel], sp.at[rel], rp_.at[rel], partner)
        pairs[rel].start()

    ahead = lax.rem(y + 1, n_y) * 2 + c
    behind = lax.rem(y + n_y - 1, n_y) * 2 + c
    lo, hi = pl.ds(0, half), pl.ds(half, half)

    def both(rel, rows):
        return part[rel, rows, own_cols] + pair[rel, rows, :]

    send_a = to_tensor(anti.at[lo], hop_a, sh.at[0], rh.at[0], ahead)
    send_b = to_tensor(anti.at[hi], hop_b, sh.at[1], rh.at[1], behind)
    fwd_hi = to_tensor(fwd.at[hi], got_f.at[hi], sh.at[2], rh.at[2], ahead)
    bwd_lo = to_tensor(bwd.at[lo], got_b.at[lo], sh.at[3], rh.at[3], behind)
    fwd_lo = to_tensor(fwd.at[lo], got_f.at[lo], sh.at[4], rh.at[4], ahead)
    bwd_hi = to_tensor(bwd.at[hi], got_b.at[hi], sh.at[5], rh.at[5], behind)

    pairs[2].wait_recv()
    anti[...] = both(2, slice(None)).astype(jnp.bfloat16)
    send_a.start()
    send_b.start()
    pairs[1].wait_recv()
    fwd[hi, :] = both(1, hi).astype(jnp.bfloat16)
    fwd_hi.start()
    pairs[3].wait_recv()
    bwd[lo, :] = both(3, lo).astype(jnp.bfloat16)
    bwd_lo.start()
    send_a.wait_recv()
    fwd[lo, :] = (both(1, lo) + hop_a[...].astype(jnp.float32)).astype(jnp.bfloat16)
    fwd_lo.start()
    send_b.wait_recv()
    bwd[hi, :] = (both(3, hi) + hop_b[...].astype(jnp.float32)).astype(jnp.bfloat16)
    bwd_hi.start()

    wait_all(first, "recv")

    def serve(d, _):
        for s in range(SLOTS):
            code = row_ref[0, d * rp + s * upr]
            outb[d * no + s] = held[lax.div(code, owned) * nt + lax.rem(code, owned)]
        return 0

    lax.fori_loop(0, n_dp, serve, 0)
    source = jnp.concatenate([held[o * nt + k + u] for o in range(n_dp) for u in range(nu)], axis=0)
    shape = (n_dp * rp, n_dp * nu * ROWS)
    code = col_ref[:, 0:1]
    shift = owned.bit_length() - 1
    src = lax.shift_right_logical(code, shift) * (nu * ROWS) + (code & (owned - 1)) * upr
    src = src + iota((n_dp * rp, 1), 0) % upr
    pickup = jnp.where(src == iota(shape, 1), 1.0, 0.0).astype(jnp.bfloat16)
    ups = jnp.dot(pickup, source, preferred_element_type=jnp.float32).reshape(n_dp, rp, LANES)
    if rp < nuo * ROWS:
        ups = jnp.concatenate([ups, jnp.zeros((n_dp, nuo * ROWS - rp, LANES), jnp.float32)], axis=1)
    ups = ups.astype(jnp.bfloat16)
    for d in range(n_dp):
        for u in range(nuo):
            outb[d * no + SLOTS + u] = ups[d, u * ROWS : (u + 1) * ROWS, :]
    start_all(second)

    def keep2(b, _):
        land[dp * no + b] = outb[dp * no + b]
        return 0

    lax.fori_loop(0, no, keep2, 0)
    wait_all(second, "recv")

    for i in range(n_dp):
        rg, cg = divmod(i, ncg)
        for s in range(SLOTS):
            panel[s, rg * ROWS : (rg + 1) * ROWS, cg * LANES : (cg + 1) * LANES] = land[i * no + s]

    per = n_t // SLOTS
    for s in range(SLOTS):
        low = lax.dot_general(
            panel[s], tok[s * seq : (s + 1) * seq, :], (((1,), (1,)), ((), ())),
            preferred_element_type=jnp.float32,
        )
        for h in range(per):
            lowp[s * per + h] = low[:, h * tb : (h + 1) * tb]

    def spread(src, dst, send_sem, recv_sem, step, by_peer):
        peer = lax.rem(t + step, n_t)
        return to_tensor(
            src.at[peer] if by_peer else src, dst.at[t], send_sem.at[step], recv_sem.at[step], peer
        )

    scatter = [spread(lowp, lowr, s3, r3, q, True) for q in range(1, n_t)]
    for cp in scatter:
        cp.start()
    lowr[t] = lowp[t]
    source = jnp.concatenate([land[i * no + SLOTS + u] for i in range(n_dp) for u in range(nuo)], axis=0)
    shape = (SLOTS * rank, n_dp * nuo * ROWS)
    r = iota(shape, 0)
    src = (r % rank) // upr * (nuo * ROWS) + r // rank * upr + r % upr
    perm = jnp.where(src == iota(shape, 1), 1.0, 0.0).astype(jnp.bfloat16)
    ups = jnp.dot(perm, source, preferred_element_type=jnp.float32).astype(jnp.bfloat16)
    for cp in scatter:
        cp.wait_recv()
    total = lowr[0]
    for q in range(1, n_t):
        total = total + lowr[q]
    lowb[...] = total.astype(jnp.bfloat16)
    gather = [spread(lowb, lowa, s4, r4, q, False) for q in range(1, n_t)]
    for cp in gather:
        cp.start()
    lowa[t] = total.astype(jnp.bfloat16)

    pairs[0].wait_recv()
    fwd_hi.wait_recv()
    bwd_lo.wait_recv()
    fwd_lo.wait_recv()
    bwd_hi.wait_recv()
    for cp in gather:
        cp.wait_recv()
    for b in range(n_t):
        rows = pl.ds(b * tb, tb)
        delta = lax.dot_general(
            lowa[b], ups[b // per * rank : (b // per + 1) * rank, :], (((0,), (0,)), ((), ())),
            preferred_element_type=jnp.float32,
        )
        base = both(0, rows) + got_f[rows, :].astype(jnp.float32) + got_b[rows, :].astype(jnp.float32)
        out_ref[rows, :] = (base + adapter_scale * delta).astype(jnp.bfloat16)

    wait_all(first, "send")
    wait_all(second, "send")
    for rel in range(4):
        pairs[rel].wait_send()
    for cp in (send_a, send_b, fwd_hi, bwd_lo, fwd_lo, bwd_hi, *scatter, *gather):
        cp.wait_send()


def gather_ids(n_dp, owned, upr, ids, table):
    n = n_dp * SLOTS * upr
    return pl.pallas_call(
        functools.partial(ids_kernel, n_dp, owned, upr),
        name="gather_ids",
        out_shape=(
            jax.ShapeDtypeStruct((8, n), jnp.int32),
            jax.ShapeDtypeStruct((n, LANES), jnp.int32),
        ),
        in_specs=[pl.BlockSpec(memory_space=pltpu.SMEM), pl.BlockSpec(memory_space=pltpu.VMEM)],
        out_specs=(pl.BlockSpec(memory_space=pltpu.VMEM), pl.BlockSpec(memory_space=pltpu.VMEM)),
        scratch_shapes=[
            pltpu.VMEM((SLOTS * upr, LANES), jnp.int32),
            pltpu.VMEM((n_dp, SLOTS * upr, LANES), jnp.int32),
            pltpu.SemaphoreType.DMA((n_dp,)),
            pltpu.SemaphoreType.DMA((n_dp,)),
        ],
        compiler_params=pltpu.CompilerParams(collective_id=0, has_side_effects=True),
    )(ids, table)


def project(n_dp, n_t, k, upr, collective_id, rows_info, cols_info, tokens, weight, down_t, up):
    n_rows, width = tokens.shape
    owned, rank, columns = up.shape
    nt = k + -(-upr * k // ROWS)
    nuo = -(-SLOTS * upr // ROWS)
    no = SLOTS + nuo
    kk = -(-upr * k // ROWS) * ROWS // upr
    bf, f32 = jnp.bfloat16, jnp.float32
    dma = pltpu.SemaphoreType.DMA
    half, tb = n_rows // 2, n_rows // n_t
    anywhere = pl.BlockSpec(memory_space=pl.ANY)
    return pl.pallas_call(
        functools.partial(main_kernel, n_dp, n_t, k, upr),
        name=f"project_{k}",
        out_shape=jax.ShapeDtypeStruct((n_rows, columns), bf),
        in_specs=[
            pl.BlockSpec(memory_space=pltpu.SMEM),
            pl.BlockSpec(memory_space=pltpu.VMEM),
            anywhere, anywhere, anywhere, anywhere,
        ],
        out_specs=pl.BlockSpec(memory_space=pltpu.VMEM),
        scratch_shapes=[
            pltpu.VMEM((n_rows, width), bf),
            pltpu.VMEM(weight.shape, bf),
            pltpu.VMEM(down_t.shape, bf),
            pltpu.VMEM(up.shape, bf),
            pltpu.VMEM((kk * rank, LANES), bf),
            pltpu.VMEM((n_dp * nt, ROWS, LANES), bf),
            pltpu.VMEM((n_dp * nt, ROWS, LANES), bf),
            pltpu.VMEM((n_dp * no, ROWS, LANES), bf),
            pltpu.VMEM((n_dp * no, ROWS, LANES), bf),
            pltpu.VMEM((4, n_rows, 2 * LANES), f32),
            pltpu.VMEM((4, n_rows, LANES), f32),
            pltpu.VMEM((n_rows, LANES), bf),
            pltpu.VMEM((n_rows, LANES), bf),
            pltpu.VMEM((n_rows, LANES), bf),
            pltpu.VMEM((half, LANES), bf),
            pltpu.VMEM((half, LANES), bf),
            pltpu.VMEM((n_rows, LANES), bf),
            pltpu.VMEM((n_rows, LANES), bf),
            pltpu.VMEM((SLOTS, rank, width), bf),
            pltpu.VMEM((n_t, rank, tb), f32),
            pltpu.VMEM((n_t, rank, tb), f32),
            pltpu.VMEM((rank, tb), bf),
            pltpu.VMEM((n_t, rank, tb), bf),
            dma((4,)),
            dma((n_dp,)), dma((n_dp,)),
            dma((n_dp,)), dma((n_dp,)),
            dma((4,)), dma((4,)),
            dma((6,)), dma((6,)),
            dma((n_t,)), dma((n_t,)),
            dma((n_t,)), dma((n_t,)),
        ],
        compiler_params=pltpu.CompilerParams(
            collective_id=collective_id, has_side_effects=True, vmem_limit_bytes=VMEM_LIMIT
        ),
    )(rows_info, cols_info, tokens, weight, down_t, up)


FEW = 6


def shards(
    tokens,
    base_value_weight,
    adapter_down_weight,
    adapter_up_weight,
    request_adapter_index,
    storage_index_table,
):
    n_dp, n_t = lax.axis_size("dp"), lax.axis_size("tensor")
    owned, width, rank = adapter_down_weight.shape
    upr = rank // n_dp
    down_t = jnp.swapaxes(adapter_down_weight, 1, 2)
    rows_info, cols_info = gather_ids(
        n_dp, owned, upr, request_adapter_index, storage_index_table.reshape(1, -1)
    )
    operands = (rows_info, cols_info, tokens, base_value_weight, down_t, adapter_up_weight)
    return lax.cond(
        rows_info[2, 0] <= FEW,
        functools.partial(project, n_dp, n_t, FEW, upr, 1),
        functools.partial(project, n_dp, n_t, owned, upr, 2),
        *operands,
    )


def solution(mesh):
    return jax.shard_map(
        shards,
        mesh=mesh,
        in_specs=(
            P("dp", "tensor"),
            P("tensor", None),
            P("dp", "tensor", None),
            P("dp", None, "tensor"),
            P("dp"),
            P(),
        ),
        out_specs=P("dp", "tensor"),
        check_vma=False,
    )
```

```python
import functools

import jax
import jax.numpy as jnp
from jax import lax
from jax.experimental import pallas as pl
from jax.experimental.pallas import tpu as pltpu
from jax.sharding import PartitionSpec as P

MESH = pl.DeviceIdType.MESH
adapter_scale = 0.5
LANES = 128
ROWS = 16
SLOTS = 4
VMEM_LIMIT = 60 * 1024 * 1024


def iota(shape, axis):
    return lax.broadcasted_iota(jnp.int32, shape, axis)


def visit(q, n):
    half = q // 2 + 1
    return half + (q % 2) * (n - 2 * half)


def ids_kernel(n_dp, owned, upr, counts, ids_ref, table_ref, row_ref, col_ref, way_ref, mine, every, send_sem, recv_sem):
    dp = lax.axis_index("dp")
    shift = owned.bit_length() - 1
    rp = SLOTS * upr
    slot = iota((rp, LANES), 0) // upr
    tile = jnp.zeros((rp, LANES), jnp.int32)
    for s in range(SLOTS):
        tile = jnp.where(slot == s, ids_ref[s], tile)
    mine[...] = tile
    every[dp] = tile

    barrier = pltpu.get_barrier_semaphore()

    def greet(q, _):
        peer = lax.rem(dp + visit(n_dp - 2 - q, n_dp), n_dp)
        pl.semaphore_signal(barrier, inc=1, device_id={"dp": peer}, device_id_type=MESH)
        return 0

    lax.fori_loop(0, n_dp - 1, greet, 0)
    pl.semaphore_wait(barrier, n_dp - 1)

    def push(step):
        return pltpu.make_async_remote_copy(
            src_ref=mine,
            dst_ref=every.at[dp],
            send_sem=send_sem.at[step],
            recv_sem=recv_sem.at[step],
            device_id={"dp": lax.rem(dp + step, n_dp)},
            device_id_type=MESH,
        )

    def go(q, _):
        push(visit(n_dp - 2 - q, n_dp)).start()
        return 0

    def come(step, _):
        push(step).wait()
        return 0

    lax.fori_loop(0, n_dp - 1, go, 0)
    lax.fori_loop(1, n_dp, come, 0)

    n = n_dp * rp
    ids = every[...].reshape(n, LANES)
    blocks = table_ref.shape[1] // LANES
    lane = iota((n, LANES), 1)
    found = jnp.zeros((n, LANES), jnp.int32)
    for b in range(blocks):
        row = table_ref[:, b * LANES : (b + 1) * LANES]
        hit = ids == lane + b * LANES
        found += jnp.where(hit, row, 0)
    pos = jnp.sum(found, axis=1, keepdims=True)
    owner = lax.shift_right_logical(pos, shift)
    before = jnp.zeros((n, LANES), jnp.int32)
    among = jnp.zeros((n, LANES), jnp.int32)
    for b in range(blocks):
        at = lane + b * LANES
        needed = jnp.max(jnp.where(pos == at, 1, 0), axis=0, keepdims=True)
        same = jnp.where(lax.shift_right_logical(at, shift) == owner, needed, 0)
        among += same
        before += jnp.where(at < pos, same, 0)
    count = jnp.sum(among, axis=1, keepdims=True)
    rank = jnp.sum(before, axis=1, keepdims=True)
    code = owner * owned + rank
    col_ref[...] = jnp.broadcast_to(code, (n, LANES))
    for b in range(n // LANES):
        diag = iota((n, LANES), 0) == lane + b * LANES
        row_ref[0:1, b * LANES : (b + 1) * LANES] = jnp.sum(jnp.where(diag, code, 0), axis=0, keepdims=True)
    own = jnp.where((owner == dp) & (rank == lane), pos - dp * owned, 0)
    row_ref[1:2, 0:LANES] = jnp.max(own, axis=0, keepdims=True)
    most = jnp.max(count, axis=0, keepdims=True)
    way_ref[...] = sum(jnp.where(most > c, 1, 0) for c in counts[:-1])


def main_kernel(
    n_dp, n_t, k, upr,
    row_ref, col_ref, tok_hbm, w_hbm, down_hbm, up_hbm, out_ref,
    tok, w, down, up, upt, stage, held, outb, land, part, pair, anti, fwd, bwd, hop_a, hop_b, got_f, got_b,
    panel, lown, lowp, lowr, lowb, lowa,
    load_sem, s1, r1, s2, r2, s5, r5, sp, rp_, sh, rh, s3, r3, s4, r4,
):
    dp = lax.axis_index("dp")
    t = lax.axis_index("tensor")
    y, c = t // 2, t % 2
    n_y = n_t // 2
    n_rows, width = tok.shape
    owned, rank, _ = down.shape
    seq = n_rows // SLOTS
    ncg = width // LANES
    nu = -(-upr * k // ROWS)
    nt = k + nu
    nuo = -(-SLOTS * upr // ROWS)
    no = SLOTS + nuo
    rp = SLOTS * upr
    half = n_rows // 2
    tb = n_rows // (2 * n_t)

    loads = [
        pltpu.make_async_copy(a, b, load_sem.at[i])
        for i, (a, b) in enumerate(((down_hbm, down), (up_hbm, up), (tok_hbm, tok), (w_hbm, w)))
    ]
    for cp in loads:
        cp.start()

    barrier = pltpu.get_barrier_semaphore()

    def greet_dp(q, _):
        pl.semaphore_signal(barrier, inc=1, device_id={"dp": lax.rem(dp + q, n_dp)}, device_id_type=MESH)
        return 0

    def greet_t(q, _):
        pl.semaphore_signal(barrier, inc=1, device_id={"tensor": lax.rem(t + q, n_t)}, device_id_type=MESH)
        return 0

    lax.fori_loop(1, n_dp, greet_dp, 0)
    lax.fori_loop(1, n_t, greet_t, 0)

    kk = nu * ROWS // upr
    m = n_dp * nu * ROWS
    r = iota((m, 1), 0)
    src = (r % (nu * ROWS)) // upr * rank + r // (nu * ROWS) * upr + r % upr
    perm = jnp.where(src == iota((m, kk * rank), 1), 1.0, 0.0).astype(jnp.bfloat16)
    loads[0].wait()
    loads[1].wait()

    def pick(j, _):
        which = row_ref[1, j]
        for i in range(n_dp):
            rg, cg = divmod(i, ncg)
            stage[i * nt + j] = down[which, rg * ROWS : (rg + 1) * ROWS, cg * LANES : (cg + 1) * LANES]
        return 0

    lax.fori_loop(0, k, pick, 0)
    for j in range(kk):
        upt[j * rank : (j + 1) * rank, :] = up[row_ref[1, min(j, k - 1)]]
    ups = jnp.dot(perm, upt[0 : kk * rank, :], preferred_element_type=jnp.float32).astype(jnp.bfloat16)
    for i in range(n_dp):
        for u in range(nu):
            b = i * nu + u
            stage[i * nt + k + u] = ups[b * ROWS : (b + 1) * ROWS, :]

    pl.semaphore_wait(barrier, n_dp - 1 + n_t - 1)

    def exchange(src_ref, dst_ref, size, at, amount, send_sem, recv_sem, step):
        peer = lax.rem(dp + step, n_dp)
        return pltpu.make_async_remote_copy(
            src_ref=src_ref.at[pl.ds(peer * size + at, amount)],
            dst_ref=dst_ref.at[pl.ds(dp * size + at, amount)],
            send_sem=send_sem.at[step],
            recv_sem=recv_sem.at[step],
            device_id={"dp": peer},
            device_id_type=MESH,
        )

    def start_all(make):
        def body(q, _):
            make(visit(q, n_dp)).start()
            return 0

        lax.fori_loop(0, n_dp - 1, body, 0)

    def wait_all(make, kind):
        def body(q, _):
            cp = make(visit(q, n_dp))
            cp.wait_recv() if kind == "recv" else cp.wait_send()
            return 0

        lax.fori_loop(0, n_dp - 1, body, 0)

    first = functools.partial(exchange, stage, held, nt, 0, nt, s1, r1)
    early = SLOTS // 2
    second = [
        functools.partial(exchange, outb, land, no, 0, early, s2, r2),
        functools.partial(exchange, outb, land, no, early, no - early, s5, r5),
    ]

    start_all(first)

    def keep1(b, _):
        held[dp * nt + b] = stage[dp * nt + b]
        return 0

    lax.fori_loop(0, nt, keep1, 0)

    loads[2].wait()
    loads[3].wait()

    def to_tensor(src_ref, dst_ref, send_sem, recv_sem, peer):
        return pltpu.make_async_remote_copy(
            src_ref=src_ref, dst_ref=dst_ref, send_sem=send_sem, recv_sem=recv_sem,
            device_id={"tensor": peer}, device_id_type=MESH,
        )

    partner = t + 1 - 2 * c
    own_cols = pl.ds(pl.multiple_of(c * LANES, LANES), LANES)
    other_cols = pl.ds(pl.multiple_of((1 - c) * LANES, LANES), LANES)
    mb = 256
    pairs = {}
    for rel in (2, 1, 3, 0):
        target = lax.rem(y + rel, n_y)
        cols = pl.ds(pl.multiple_of(target * 2 * LANES, 2 * LANES), 2 * LANES)

        def block(i, _, rel=rel, cols=cols):
            rows = pl.ds(pl.multiple_of(i * mb, mb), mb)
            part[rel, rows, :] = jnp.dot(tok[rows, :], w[:, cols], preferred_element_type=jnp.float32)
            return 0

        lax.fori_loop(0, n_rows // mb, block, 0)
        pairs[rel] = to_tensor(part.at[rel, :, other_cols], pair.at[rel], sp.at[rel], rp_.at[rel], partner)
        pairs[rel].start()

    ahead = lax.rem(y + 1, n_y) * 2 + c
    behind = lax.rem(y + n_y - 1, n_y) * 2 + c
    lo, hi = pl.ds(0, half), pl.ds(half, half)

    def both(rel, rows):
        return part[rel, rows, own_cols] + pair[rel, rows, :]

    send_a = to_tensor(anti.at[lo], hop_a, sh.at[0], rh.at[0], ahead)
    send_b = to_tensor(anti.at[hi], hop_b, sh.at[1], rh.at[1], behind)
    fwd_hi = to_tensor(fwd.at[hi], got_f.at[hi], sh.at[2], rh.at[2], ahead)
    bwd_lo = to_tensor(bwd.at[lo], got_b.at[lo], sh.at[3], rh.at[3], behind)
    fwd_lo = to_tensor(fwd.at[lo], got_f.at[lo], sh.at[4], rh.at[4], ahead)
    bwd_hi = to_tensor(bwd.at[hi], got_b.at[hi], sh.at[5], rh.at[5], behind)

    pairs[2].wait_recv()
    anti[...] = both(2, slice(None)).astype(jnp.bfloat16)
    send_a.start()
    send_b.start()
    pairs[1].wait_recv()
    fwd[hi, :] = both(1, hi).astype(jnp.bfloat16)
    fwd_hi.start()
    pairs[3].wait_recv()
    bwd[lo, :] = both(3, lo).astype(jnp.bfloat16)
    bwd_lo.start()
    send_a.wait_recv()
    fwd[lo, :] = (both(1, lo) + hop_a[...].astype(jnp.float32)).astype(jnp.bfloat16)
    fwd_lo.start()
    send_b.wait_recv()
    bwd[hi, :] = (both(3, hi) + hop_b[...].astype(jnp.float32)).astype(jnp.bfloat16)
    bwd_hi.start()

    shape = (n_dp * rp, n_dp * nu * ROWS)
    code = col_ref[:, 0:1]
    shift = owned.bit_length() - 1
    src = lax.shift_right_logical(code, shift) * (nu * ROWS) + (code & (owned - 1)) * upr
    src = src + iota((n_dp * rp, 1), 0) % upr
    pickup = jnp.where(src == iota(shape, 1), 1.0, 0.0).astype(jnp.bfloat16)
    r = iota((SLOTS * rank, 1), 0)
    src = (r % rank) // upr * (nuo * ROWS) + r // rank * upr + r % upr
    arrange = jnp.where(src == iota((SLOTS * rank, n_dp * nuo * ROWS), 1), 1.0, 0.0).astype(jnp.bfloat16)
    wait_all(first, "recv")

    def serve(slots):
        def body(d, _):
            for s in slots:
                code = row_ref[0, d * rp + s * upr]
                outb[d * no + s] = held[lax.shift_right_logical(code, shift) * nt + (code & (owned - 1))]
            return 0

        lax.fori_loop(0, n_dp, body, 0, unroll=4)

    serve(range(early))
    start_all(second[0])
    serve(range(early, SLOTS))
    source = jnp.concatenate([held[o * nt + k + u] for o in range(n_dp) for u in range(nu)], axis=0)
    ups = jnp.dot(pickup, source, preferred_element_type=jnp.float32).reshape(n_dp, rp, LANES)
    if rp < nuo * ROWS:
        ups = jnp.concatenate([ups, jnp.zeros((n_dp, nuo * ROWS - rp, LANES), jnp.float32)], axis=1)
    ups = ups.astype(jnp.bfloat16)
    for d in range(n_dp):
        for u in range(nuo):
            outb[d * no + SLOTS + u] = ups[d, u * ROWS : (u + 1) * ROWS, :]
    start_all(second[1])

    def keep2(b, _):
        land[dp * no + b] = outb[dp * no + b]
        return 0

    lax.fori_loop(0, no, keep2, 0)

    def spread(src, dst, send_sem, recv_sem, g, step, by_peer):
        peer = lax.rem(t + step, n_t)
        return to_tensor(
            src.at[g, peer] if by_peer else src.at[g], dst.at[g, t], send_sem.at[g, step], recv_sem.at[g, step], peer
        )

    scatter = [[spread(lowp, lowr, s3, r3, g, q, True) for q in range(1, n_t)] for g in range(2)]
    gather = [[spread(lowb, lowa, s4, r4, g, q, False) for q in range(1, n_t)] for g in range(2)]
    per = n_t // early

    def low_part(g):
        for s in range(g * early, (g + 1) * early):
            for i in range(n_dp):
                rg, cg = divmod(i, ncg)
                panel[s, rg * ROWS : (rg + 1) * ROWS, cg * LANES : (cg + 1) * LANES] = land[i * no + s]
            low = lax.dot_general(
                panel[s], tok[s * seq : (s + 1) * seq, :], (((1,), (1,)), ((), ())),
                preferred_element_type=jnp.float32,
            )
            for h in range(per):
                b = (s - g * early) * per + h
                lown[g, b] = low[:, h * tb : (h + 1) * tb]
                lowp[g, b] = low[:, h * tb : (h + 1) * tb].astype(jnp.bfloat16)
        for cp in scatter[g]:
            cp.start()

    def low_total(g):
        for cp in scatter[g]:
            cp.wait_recv()
        total = lown[g, t]
        for q in range(1, n_t):
            total = total + lowr[g, lax.rem(t + q, n_t)].astype(jnp.float32)
        lowb[g] = total.astype(jnp.bfloat16)
        for cp in gather[g]:
            cp.start()
        lowa[g, t] = total.astype(jnp.bfloat16)

    def finish(g):
        for cp in gather[g]:
            cp.wait_recv()
        for b in range(n_t):
            s = g * early + b // per
            rows = pl.ds((g * n_t + b) * tb, tb)
            delta = lax.dot_general(
                lowa[g, b], ups[s * rank : (s + 1) * rank, :], (((0,), (0,)), ((), ())),
                preferred_element_type=jnp.float32,
            )
            base = both(0, rows) + got_f[rows, :].astype(jnp.float32) + got_b[rows, :].astype(jnp.float32)
            out_ref[rows, :] = (base + adapter_scale * delta).astype(jnp.bfloat16)

    wait_all(second[0], "recv")
    low_part(0)
    low_total(0)
    wait_all(second[1], "recv")
    low_part(1)
    source = jnp.concatenate([land[i * no + SLOTS + u] for i in range(n_dp) for u in range(nuo)], axis=0)
    ups = jnp.dot(arrange, source, preferred_element_type=jnp.float32).astype(jnp.bfloat16)
    pairs[0].wait_recv()
    fwd_hi.wait_recv()
    bwd_lo.wait_recv()
    fwd_lo.wait_recv()
    bwd_hi.wait_recv()
    finish(0)
    low_total(1)
    finish(1)

    wait_all(first, "send")
    for part_of in second:
        wait_all(part_of, "send")
    for rel in range(4):
        pairs[rel].wait_send()
    for cp in (send_a, send_b, fwd_hi, bwd_lo, fwd_lo, bwd_hi, *scatter[0], *scatter[1], *gather[0], *gather[1]):
        cp.wait_send()


def gather_ids(n_dp, owned, upr, counts, ids, table):
    n = n_dp * SLOTS * upr
    return pl.pallas_call(
        functools.partial(ids_kernel, n_dp, owned, upr, counts),
        name="gather_ids",
        out_shape=(
            jax.ShapeDtypeStruct((8, n), jnp.int32),
            jax.ShapeDtypeStruct((n, LANES), jnp.int32),
            jax.ShapeDtypeStruct((1, 1), jnp.int32),
        ),
        in_specs=[pl.BlockSpec(memory_space=pltpu.SMEM), pl.BlockSpec(memory_space=pltpu.VMEM)],
        out_specs=(pl.BlockSpec(memory_space=pltpu.VMEM),) * 3,
        scratch_shapes=[
            pltpu.VMEM((SLOTS * upr, LANES), jnp.int32),
            pltpu.VMEM((n_dp, SLOTS * upr, LANES), jnp.int32),
            pltpu.SemaphoreType.DMA((n_dp,)),
            pltpu.SemaphoreType.DMA((n_dp,)),
        ],
        compiler_params=pltpu.CompilerParams(collective_id=0, has_side_effects=True),
    )(ids, table)


def project(n_dp, n_t, k, upr, collective_id, rows_info, cols_info, tokens, weight, down_t, up):
    n_rows, width = tokens.shape
    owned, rank, columns = up.shape
    nt = k + -(-upr * k // ROWS)
    nuo = -(-SLOTS * upr // ROWS)
    no = SLOTS + nuo
    kk = -(-upr * k // ROWS) * ROWS // upr
    bf, f32 = jnp.bfloat16, jnp.float32
    dma = pltpu.SemaphoreType.DMA
    half, tb = n_rows // 2, n_rows // (2 * n_t)
    anywhere = pl.BlockSpec(memory_space=pl.ANY)
    return pl.pallas_call(
        functools.partial(main_kernel, n_dp, n_t, k, upr),
        name=f"project_{k}",
        out_shape=jax.ShapeDtypeStruct((n_rows, columns), bf),
        in_specs=[
            pl.BlockSpec(memory_space=pltpu.SMEM),
            pl.BlockSpec(memory_space=pltpu.VMEM),
            anywhere, anywhere, anywhere, anywhere,
        ],
        out_specs=pl.BlockSpec(memory_space=pltpu.VMEM),
        scratch_shapes=[
            pltpu.VMEM((n_rows, width), bf),
            pltpu.VMEM(weight.shape, bf),
            pltpu.VMEM(down_t.shape, bf),
            pltpu.VMEM(up.shape, bf),
            pltpu.VMEM((kk * rank, LANES), bf),
            pltpu.VMEM((n_dp * nt, ROWS, LANES), bf),
            pltpu.VMEM((n_dp * nt, ROWS, LANES), bf),
            pltpu.VMEM((n_dp * no, ROWS, LANES), bf),
            pltpu.VMEM((n_dp * no, ROWS, LANES), bf),
            pltpu.VMEM((4, n_rows, 2 * LANES), f32),
            pltpu.VMEM((4, n_rows, LANES), f32),
            pltpu.VMEM((n_rows, LANES), bf),
            pltpu.VMEM((n_rows, LANES), bf),
            pltpu.VMEM((n_rows, LANES), bf),
            pltpu.VMEM((half, LANES), bf),
            pltpu.VMEM((half, LANES), bf),
            pltpu.VMEM((n_rows, LANES), bf),
            pltpu.VMEM((n_rows, LANES), bf),
            pltpu.VMEM((SLOTS, rank, width), bf),
            pltpu.VMEM((2, n_t, rank, tb), f32),
            pltpu.VMEM((2, n_t, rank, tb), bf),
            pltpu.VMEM((2, n_t, rank, tb), bf),
            pltpu.VMEM((2, rank, tb), bf),
            pltpu.VMEM((2, n_t, rank, tb), bf),
            dma((4,)),
            dma((n_dp,)), dma((n_dp,)),
            dma((n_dp,)), dma((n_dp,)),
            dma((n_dp,)), dma((n_dp,)),
            dma((4,)), dma((4,)),
            dma((6,)), dma((6,)),
            dma((2, n_t)), dma((2, n_t)),
            dma((2, n_t)), dma((2, n_t)),
        ],
        compiler_params=pltpu.CompilerParams(
            collective_id=collective_id, has_side_effects=True, vmem_limit_bytes=VMEM_LIMIT
        ),
    )(rows_info, cols_info, tokens, weight, down_t, up)


COUNTS = (4, 5, 6, 8)


def shards(
    tokens,
    base_value_weight,
    adapter_down_weight,
    adapter_up_weight,
    request_adapter_index,
    storage_index_table,
):
    n_dp, n_t = lax.axis_size("dp"), lax.axis_size("tensor")
    owned, width, rank = adapter_down_weight.shape
    upr = rank // n_dp
    down_t = jnp.swapaxes(adapter_down_weight, 1, 2)
    counts = (*(c for c in COUNTS if c < owned), owned)
    rows_info, cols_info, way = gather_ids(
        n_dp, owned, upr, counts, request_adapter_index, storage_index_table.reshape(1, -1)
    )
    operands = (rows_info, cols_info, tokens, base_value_weight, down_t, adapter_up_weight)
    return lax.switch(
        way[0, 0],
        [functools.partial(project, n_dp, n_t, c, upr, 1 + i) for i, c in enumerate(counts)],
        *operands,
    )


def solution(mesh):
    return jax.shard_map(
        shards,
        mesh=mesh,
        in_specs=(
            P("dp", "tensor"),
            P("tensor", None),
            P("dp", "tensor", None),
            P("dp", None, "tensor"),
            P("dp"),
            P(),
        ),
        out_specs=P("dp", "tensor"),
        check_vma=False,
    )
```
